32 devices in a mesh: dp: 8 (over z, core), row: 2 (over x), col: 2 (over y).
Axes of the slice: x: 2, y: 2, z: 4, core: 2. Of those that a mesh axis runs over, the one named last changes fastest.
Arguments:
- tokens: bfloat16 [16384, 1024], P(('dp', 'row'), 'col'), may hold values from -6 to 6
- mixer_gain: float32 [1024], P('col'), may hold values from 0.1 to 1.9
- in_weight: bfloat16 [1024, 3, 1024], P('col', None, 'row'), may hold values from -0.1875 to 0.1875
- conv_kernel: float32 [3, 1024], P(None, 'row'), may hold values from -3.5 to 3.5
- out_weight: bfloat16 [1024, 1024], P('row', 'col'), may hold values from -0.1875 to 0.1875
- ffn_gain: float32 [1024], P('col'), may hold values from 0.1 to 1.9
- ffn_weight: bfloat16 [1024, 2, 4608], P('col', None, 'row'), may hold values from -0.1875 to 0.1875
- down_weight: bfloat16 [4608, 1024], P('row', 'col'), may hold values from -0.1875 to 0.1875
- cotangent: bfloat16 [16384, 1024], P(('dp', 'row'), 'col'), may hold values from -6 to 6
Outputs:
- output: bfloat16 [16384, 1024], P(('dp', 'row'), 'col')
- d_tokens: float32 [16384, 1024], P(('dp', 'row'), 'col')
- d_mixer_gain: float32 [1024], P('col')
- d_in_weight: float32 [1024, 3, 1024], P('col', None, 'row')
- d_conv_kernel: float32 [3, 1024], P(None, 'row')
- d_out_weight: float32 [1024, 1024], P('row', 'col')
- d_ffn_gain: float32 [1024], P('col')
- d_ffn_weight: float32 [1024, 2, 4608], P('col', None, 'row')
- d_down_weight: float32 [4608, 1024], P('row', 'col')
The draws below stay inside these ranges and needn't reach their ends.
All inputs are finite; a program needn't handle non-finite values.
Results may differ from the reference program's by a relative error of at most 0.015.
Values may be sent and summed in bfloat16 or wider, within the bound.
No kernel may reach another device: no remote copies, remote signals or barrier semaphores. Data moves between devices by JAX's collectives and lax.ppermute only.
A program may use at most 320 MiB of HBM per device.

```python
import jax
import jax.numpy as jnp
from jax import lax

D = 1024
FF = 4608
LEN = 2048
TOKENS = 16384
N_DP = 8


def levels(own_key, dims, split, low, largest):
    level, own = 1.0, jax.random.fold_in(own_key, 6)
    for dim, shards_of in split:
        steps = jnp.exp(jax.random.uniform(jax.random.fold_in(own, dim), (shards_of,), jnp.float32, low / len(split), largest / len(split)))
        level = level * jnp.repeat(steps, dims[dim] // shards_of).reshape([-1 if axis == dim else 1 for axis in range(len(dims))])
    return level


def scatter_about(own_key, shape, width, limit, cuts=(), dtype=jnp.bfloat16):
    entries = jax.random.normal(own_key, shape, jnp.float32) * width
    if len(cuts) > 0:
        entries = levels(own_key, shape, cuts, -0.22, 0.18) * entries
    return jnp.clip(entries, min=-limit, max=limit).astype(dtype)


def setup_inputs(seed: int = 0) -> dict:
    seeds = jax.random.split(jax.random.key(seed), 10)
    tokens = scatter_about(seeds[0], (TOKENS, D), 1.0, 6.0, ((0, 16), (1, 2)))
    mixer_gain = jnp.clip(1.0 + 0.18 * jax.random.normal(seeds[1], (D,), jnp.float32), 0.1, 1.9)
    in_weight = scatter_about(seeds[2], (D, 3, D), D ** -0.5, 0.1875, ((0, 2), (2, 2)))
    conv_kernel = scatter_about(seeds[3], (3, D), 3 ** -0.5, 3.5, ((1, 2),), jnp.float32)
    out_weight = scatter_about(seeds[4], (D, D), D ** -0.5, 0.1875, ((0, 2), (1, 2)))
    ffn_gain = jnp.clip(1.0 + 0.18 * jax.random.normal(seeds[5], (D,), jnp.float32), 0.1, 1.9)
    ffn_weight = scatter_about(seeds[6], (D, 2, FF), D ** -0.5, 0.1875, ((0, 2), (2, 2)))
    down_weight = scatter_about(seeds[7], (FF, D), (FF // 4) ** -0.5, 0.1875, ((0, 2), (1, 2)))
    cotangent = scatter_about(seeds[8], (TOKENS, D), 1.0, 6.0, ((0, 16), (1, 2)))
    return dict(tokens=tokens, mixer_gain=mixer_gain, in_weight=in_weight, conv_kernel=conv_kernel, out_weight=out_weight, ffn_gain=ffn_gain, ffn_weight=ffn_weight, down_weight=down_weight, cotangent=cotangent)


EPS = 1e-05

def delay(value, steps):
    zeros = jnp.zeros((steps, value.shape[1]), jnp.float32)
    return jnp.concatenate([zeros, value[:-steps]], 0)

def advance(value, steps):
    zeros = jnp.zeros((steps, value.shape[1]), jnp.float32)
    return jnp.concatenate([value[steps:], zeros], 0)

def reference(tokens, mixer_gain, in_weight, conv_kernel, out_weight, ffn_gain, ffn_weight, down_weight, cotangent):
    wide_in = in_weight.reshape(D, 3 * D)
    wide_ffn = ffn_weight.reshape(D, 2 * FF)

    def one_sequence(carry, pieces):
        seq_tokens, seq_cot = pieces
        xfloat = seq_tokens.astype(jnp.float32)
        scale_one = lax.rsqrt(lax.optimization_barrier(jnp.mean(xfloat * xfloat, axis=1, keepdims=True)) + EPS)
        normed_one = xfloat * scale_one
        hidden_one = (normed_one * mixer_gain).astype(jnp.bfloat16)
        projected = jnp.dot(hidden_one, wide_in, preferred_element_type=jnp.float32)
        gate_b = projected[:, :D]
        gate_c = projected[:, D:2 * D]
        values = projected[:, 2 * D:]
        mixed_in = gate_b * values
        lag_one = delay(mixed_in, 1)
        lag_two = delay(mixed_in, 2)
        convolved = conv_kernel[2] * mixed_in + conv_kernel[1] * lag_one + conv_kernel[0] * lag_two
        mixer_out = (gate_c * convolved).astype(jnp.bfloat16)
        residual = xfloat + jnp.dot(mixer_out, out_weight, preferred_element_type=jnp.float32)
        scale_two = lax.rsqrt(lax.optimization_barrier(jnp.mean(residual * residual, axis=1, keepdims=True)) + EPS)
        normed_two = residual * scale_two
        hidden_two = (normed_two * ffn_gain).astype(jnp.bfloat16)
        gate_up = jnp.dot(hidden_two, wide_ffn, preferred_element_type=jnp.float32)
        gate_part = gate_up[:, :FF]
        up_part = gate_up[:, FF:]
        sigmoid_gate = jax.nn.sigmoid(gate_part)
        activated = (gate_part * sigmoid_gate * up_part).astype(jnp.bfloat16)
        output = (residual + jnp.dot(activated, down_weight, preferred_element_type=jnp.float32)).astype(jnp.bfloat16)
        d_act = jnp.dot(seq_cot, down_weight.T, preferred_element_type=jnp.float32)
        grad_down = jnp.dot(activated.T, seq_cot, preferred_element_type=jnp.float32)
        d_gate = d_act * up_part * sigmoid_gate * (1.0 + gate_part * (1.0 - sigmoid_gate))
        d_up = d_act * gate_part * sigmoid_gate
        d_gate_up = jnp.concatenate([d_gate, d_up], 1).astype(jnp.bfloat16)
        d_hidden_two = jnp.dot(d_gate_up, wide_ffn.T, preferred_element_type=jnp.float32)
        grad_ffn = jnp.dot(hidden_two.T, d_gate_up, preferred_element_type=jnp.float32)
        scaled_two = d_hidden_two * ffn_gain
        d_residual = seq_cot.astype(jnp.float32) + scale_two * (scaled_two - normed_two * lax.optimization_barrier(jnp.mean(scaled_two * normed_two, axis=1, keepdims=True)))
        gain_two = lax.optimization_barrier(jnp.sum(d_hidden_two * normed_two, axis=0))
        d_residual_b = d_residual.astype(jnp.bfloat16)
        d_mix = jnp.dot(d_residual_b, out_weight.T, preferred_element_type=jnp.float32)
        grad_out = jnp.dot(mixer_out.T, d_residual_b, preferred_element_type=jnp.float32)
        d_gate_c = d_mix * convolved
        d_conv = d_mix * gate_c
        d_mixed = conv_kernel[2] * d_conv + conv_kernel[1] * advance(d_conv, 1) + conv_kernel[0] * advance(d_conv, 2)
        kernel_grad = jnp.stack([lax.optimization_barrier(jnp.sum(d_conv * lag_two, axis=0)), lax.optimization_barrier(jnp.sum(d_conv * lag_one, axis=0)), lax.optimization_barrier(jnp.sum(d_conv * mixed_in, axis=0))])
        d_projected = jnp.concatenate([d_mixed * values, d_gate_c, d_mixed * gate_b], 1).astype(jnp.bfloat16)
        d_hidden_one = jnp.dot(d_projected, wide_in.T, preferred_element_type=jnp.float32)
        grad_in = jnp.dot(hidden_one.T, d_projected, preferred_element_type=jnp.float32)
        scaled_one = d_hidden_one * mixer_gain
        d_tokens = d_residual + scale_one * (scaled_one - normed_one * lax.optimization_barrier(jnp.mean(scaled_one * normed_one, axis=1, keepdims=True)))
        gain_one = lax.optimization_barrier(jnp.sum(d_hidden_one * normed_one, axis=0))
        updated = (carry[0] + gain_one, carry[1] + grad_in, carry[2] + kernel_grad, carry[3] + grad_out, carry[4] + gain_two, carry[5] + grad_ffn, carry[6] + grad_down)
        return (updated, (output, d_tokens))
    start = (jnp.zeros((D,), jnp.float32), jnp.zeros((D, 3 * D), jnp.float32), jnp.zeros((3, D), jnp.float32), jnp.zeros((D, D), jnp.float32), jnp.zeros((D,), jnp.float32), jnp.zeros((D, 2 * FF), jnp.float32), jnp.zeros((FF, D), jnp.float32))
    seq_tokens = tokens.reshape(N_DP, LEN, D)
    seq_cot = cotangent.reshape(N_DP, LEN, D)
    totals, (outputs, d_rows) = lax.scan(one_sequence, start, (seq_tokens, seq_cot))
    return (outputs.reshape(N_DP * LEN, D), d_rows.reshape(N_DP * LEN, D), totals[0], totals[1].reshape(D, 3, D), totals[2], totals[3], totals[4], totals[5].reshape(D, 2, FF), totals[6])
```

```python
import jax
import jax.numpy as jnp
from jax import lax
from jax.sharding import PartitionSpec as P

EPS = 1e-05
HALF = jnp.bfloat16


def dense(left, right):
    return jnp.dot(left, right, preferred_element_type=jnp.float32)


def dense_nt(left, right):
    return lax.dot_general(left, right, (((1,), (1,)), ((), ())), preferred_element_type=jnp.float32)


def dense_tn(left, right):
    return lax.dot_general(left, right, (((0,), (0,)), ((), ())), preferred_element_type=jnp.float32)


def pull(value, axis, k):
    size = lax.axis_size(axis)
    return lax.ppermute(value, axis, [((i + k) % size, i) for i in range(size)])


def push(value, axis, k):
    return pull(value, axis, -k)


def swap(value):
    return lax.ppermute(value, "dp", [(i, i ^ 1) for i in range(lax.axis_size("dp"))])


def gather(value, axis):
    return [value] + [pull(value, axis, k) for k in range(1, lax.axis_size(axis))]


def narrow(value):
    return lax.reduce_precision(value, 8, 7).astype(HALF)


def wide(value):
    return value.astype(jnp.float32)


def to_rows(block):
    size, mine = lax.axis_size("col"), lax.axis_index("col")
    count = block.shape[0] // size
    pieces = []
    for k in range(size):
        piece = lax.dynamic_slice_in_dim(block, ((mine - k) % size) * count, count, 0)
        pieces.append(pull(piece, "col", k) if k else piece)
    return jnp.concatenate(pieces, 1)


def from_rows(value):
    size, mine = lax.axis_size("col"), lax.axis_index("col")
    count, width = value.shape[0], value.shape[1] // size
    result = jnp.zeros((count * size, width), value.dtype)
    for k in range(size):
        piece = value[:, k * width : (k + 1) * width]
        piece = push(piece, "col", k) if k else piece
        result = lax.dynamic_update_slice_in_dim(result, piece, ((mine - k) % size) * count, 0)
    return result


def scatter(pieces, axis):
    total = wide(pieces[0])
    for k in range(1, len(pieces)):
        total = total + wide(push(pieces[k], axis, k))
    return total


def column_pieces(value):
    size = lax.axis_size("col")
    width = value.shape[1] // size
    return [value[:, k * width : (k + 1) * width] for k in range(size)]


def row_pieces(value):
    size = lax.axis_size("col")
    height = value.shape[0] // size
    return [value[k * height : (k + 1) * height] for k in range(size)]


def chips_total(value):
    count = lax.axis_size("dp") // 2
    chip = lax.axis_index("dp") // 2
    middle = count // 2

    def move(sent, routes):
        return lax.ppermute(sent, "dp", [(2 * a + c, 2 * b + c) for a, b in routes for c in range(2)])

    total = narrow(value)
    if count == 1:
        return total
    for t in range(count - middle - 1):
        routes = [(count - 1 - t, count - 2 - t)]
        if t + 1 <= middle - 1:
            routes.append((t, t + 1))
        total = narrow(wide(total) + wide(move(total, routes)))
    total = narrow(wide(total) + wide(move(total, [(middle - 1, middle), (middle, middle - 1)])))
    for t in range(count - middle - 1):
        routes = [(middle + t, middle + t + 1)]
        if middle - 2 - t >= 0:
            routes.append((middle - 1 - t, middle - 2 - t))
        arrived = move(total, routes)
        taken = (chip == middle + t + 1) | (chip == middle - 2 - t)
        total = jnp.where(taken, arrived, total)
    return total


def both_halves(mine, axis):
    other = swap(mine)
    first = lax.axis_index("dp") % 2 == 0
    mine, other = wide(mine), wide(other)
    return jnp.concatenate([jnp.where(first, mine, other), jnp.where(first, other, mine)], axis)


def own_half(value, axis):
    size = value.shape[axis] // 2
    return lax.dynamic_slice_in_dim(value, (lax.axis_index("dp") % 2) * size, size, axis)


def own_rows(partial):
    count = partial.shape[0] // 2
    return partial[:count] + wide(swap(narrow(partial[count:])))


def local(
    tokens,
    mixer_gain,
    in_weight,
    conv_kernel,
    out_weight,
    ffn_gain,
    ffn_weight,
    down_weight,
    cotangent,
):
    rows, cols = lax.axis_size("row"), lax.axis_size("col")
    row, col, core = lax.axis_index("row"), lax.axis_index("col"), lax.axis_index("dp") % 2
    features = tokens.shape[1] * cols
    own_tokens = to_rows(tokens)
    in_mine = jnp.concatenate([own_half(in_weight[:, j, :], 1) for j in range(3)], 1)
    in_blocks = gather(jnp.concatenate(gather(in_mine, "col"), 0), "row")
    gain_one = jnp.concatenate(gather(mixer_gain, "col"), 0)
    gain_two = jnp.concatenate(gather(ffn_gain, "col"), 0)
    kernels = gather(own_half(conv_kernel, 1), "row")
    out_blocks = gather(jnp.concatenate(gather(own_half(out_weight, 0), "col"), 1), "row")
    out_full = jnp.concatenate(out_blocks, 0)
    ffn_mine = jnp.concatenate([own_half(ffn_weight[:, j, :], 1) for j in range(2)], 1)
    ffn_full = jnp.concatenate(gather(ffn_mine, "col"), 0)
    down_full = jnp.concatenate(gather(own_half(down_weight, 0), "col"), 1)
    own_cot = to_rows(cotangent)

    def all_rows(mine):
        blocks = gather(mine, "row")
        return jnp.concatenate(blocks + [swap(block) for block in blocks], 0)

    def rows_total(partial):
        mine = own_rows(partial)
        count = mine.shape[0] // rows
        pieces = [mine[k * count : (k + 1) * count] for k in range(rows)]
        return scatter([pieces[0]] + [narrow(piece) for piece in pieces[1:]], "row")

    def rounds(value, distance):
        span = rows * cols
        route = [(i - distance, i) for i in range(span) if 0 <= i - distance < span]
        there = lax.ppermute(jnp.roll(value, row, 2), ("row", "col"), route)
        return jnp.roll(there, -row, 2)

    xfloat = wide(own_tokens)
    scale_one = lax.rsqrt(jnp.mean(xfloat * xfloat, axis=1, keepdims=True) + EPS)
    normed_one = xfloat * scale_one
    hidden_own = (normed_one * gain_one).astype(HALF)
    hidden_one = jnp.concatenate([hidden_own, swap(hidden_own)], 0)
    count = hidden_own.shape[0]
    width = kernels[0].shape[1]
    gates_b, gates_c, values, mixed = [], [], [], []
    for k in range(rows):
        projected = dense(hidden_one, in_blocks[k])
        gates_b.append(projected[:, :width])
        gates_c.append(projected[:, width : 2 * width])
        values.append(projected[:, 2 * width :])
        mixed.append((gates_b[k] * values[k]).reshape(2, count, width))
    before = rounds(jnp.stack([m[:, -2:] for m in mixed], 2), 1)
    lag_one, lag_two, convolved, mixer_out = [], [], [], []
    for k in range(rows):
        extended = jnp.concatenate([before[:, :, k], mixed[k]], 1)
        lag_one.append(extended[:, 1:-1])
        lag_two.append(extended[:, :-2])
        taps = kernels[k]
        convolved.append(taps[2] * mixed[k] + taps[1] * lag_one[k] + taps[0] * lag_two[k])
        mixer_out.append((gates_c[k] * convolved[k].reshape(2 * count, width)).astype(HALF))
    mixer_full = jnp.concatenate(mixer_out, 1)
    residual = xfloat + own_rows(dense(mixer_full, out_full))
    scale_two = lax.rsqrt(jnp.mean(residual * residual, axis=1, keepdims=True) + EPS)
    normed_two = residual * scale_two
    hidden_two = all_rows((normed_two * gain_two).astype(HALF))
    cot_rows = all_rows(own_cot)
    inner = down_full.shape[0]
    gate_part = dense(hidden_two, ffn_full[:, :inner])
    up_part = dense(hidden_two, ffn_full[:, inner:])
    sigmoid_gate = jax.nn.sigmoid(gate_part)
    activated = (gate_part * sigmoid_gate * up_part).astype(HALF)
    grad_down = chips_total(scatter(column_pieces(dense_tn(activated, cot_rows).astype(HALF)), "col"))
    grad_down = both_halves(grad_down, 0)
    output = from_rows((residual + rows_total(dense(activated, down_full))).astype(HALF))
    d_act = dense_nt(cot_rows, down_full)
    d_gate = d_act * up_part * sigmoid_gate * (1.0 + gate_part * (1.0 - sigmoid_gate))
    d_up = d_act * gate_part * sigmoid_gate
    d_gate_up = jnp.concatenate([d_gate.astype(HALF), d_up.astype(HALF)], 1)
    d_hidden_two = rows_total(dense_nt(d_gate_up, ffn_full))
    grad_ffn = chips_total(scatter(row_pieces(dense_tn(hidden_two, d_gate_up).astype(HALF)), "col"))
    grad_ffn = jnp.stack([both_halves(grad_ffn[:, :inner], 1), both_halves(grad_ffn[:, inner:], 1)], 1)
    scaled_two = d_hidden_two * gain_two
    inner_two = jnp.mean(scaled_two * normed_two, axis=1, keepdims=True)
    d_residual = wide(own_cot) + scale_two * (scaled_two - normed_two * inner_two)
    gain_two_part = jnp.sum(d_hidden_two * normed_two, axis=0)
    dres_own = d_residual.astype(HALF)
    dres = jnp.concatenate([dres_own, swap(dres_own)], 0)
    d_mix = dense_nt(dres, out_full)
    grad_out = dense_tn(mixer_full, dres).astype(HALF)
    grad_out = scatter([grad_out[k * width : (k + 1) * width] for k in range(rows)], "row").astype(HALF)
    grad_out = both_halves(chips_total(scatter(column_pieces(grad_out), "col")), 0)
    d_gate_c, d_conv = [], []
    for k in range(rows):
        part = d_mix[:, k * width : (k + 1) * width]
        d_gate_c.append(part * convolved[k].reshape(2 * count, width))
        d_conv.append((part * gates_c[k]).reshape(2, count, width))
    after = rounds(jnp.stack([d[:, :2] for d in d_conv], 2), -1)
    kernel_part = jnp.zeros((3, rows, 2, width), jnp.float32)
    d_projected = []
    for k in range(rows):
        extended = jnp.concatenate([d_conv[k], after[:, :, k]], 1)
        taps = kernels[k]
        d_mixed = taps[2] * d_conv[k] + taps[1] * extended[:, 1:-1] + taps[0] * extended[:, 2:]
        d_mixed = d_mixed.reshape(2 * count, width)
        sums = jnp.stack([jnp.sum(d_conv[k] * lag, axis=(0, 1)) for lag in (lag_two[k], lag_one[k], mixed[k])])
        kernel_part = lax.dynamic_update_slice(
            kernel_part, sums[:, None, None], (0, (row + k) % rows, core, 0)
        )
        d_projected.append(
            jnp.concatenate([d_mixed * values[k], d_gate_c[k], d_mixed * gates_b[k]], 1).astype(HALF)
        )
    d_hidden_one = sum(dense_nt(d_projected[k], in_blocks[k]) for k in range(rows))
    d_hidden_one = own_rows(d_hidden_one)
    grad_in = scatter([dense_tn(hidden_one, d_projected[k]).astype(HALF) for k in range(rows)], "row").astype(HALF)
    grad_in = chips_total(scatter(row_pieces(grad_in), "col"))
    grad_in = jnp.stack([both_halves(grad_in[:, j * width : (j + 1) * width], 1) for j in range(3)], 1)
    scaled_one = d_hidden_one * gain_one
    inner_one = jnp.mean(scaled_one * normed_one, axis=1, keepdims=True)
    d_tokens = d_residual + scale_one * (scaled_one - normed_one * inner_one)
    gain_one_part = jnp.sum(d_hidden_one * normed_one, axis=0)
    d_tokens = wide(from_rows(narrow(d_tokens)))
    own_width = mixer_gain.shape[0]
    gains = jnp.stack([gain_one_part, gain_two_part]).reshape(2, cols, own_width)
    gains = jnp.roll(gains, col, 1).reshape(2, features)
    small = jnp.concatenate([gains, kernel_part.reshape(3, rows * 2 * width)], 0)
    small = lax.psum(small, ("dp", "row", "col"))
    gains = lax.dynamic_slice_in_dim(small[:2], col * own_width, own_width, 1)
    grad_kernel = lax.dynamic_slice_in_dim(small[2:], row * 2 * width, 2 * width, 1)
    return (
        output,
        d_tokens,
        gains[0],
        grad_in,
        grad_kernel,
        grad_out,
        gains[1],
        grad_ffn,
        grad_down,
    )


def solution(mesh):
    in_specs = (
        P(("dp", "row"), "col"),
        P("col"),
        P("col", None, "row"),
        P(None, "row"),
        P("row", "col"),
        P("col"),
        P("col", None, "row"),
        P("row", "col"),
        P(("dp", "row"), "col"),
    )
    out_specs = (
        P(("dp", "row"), "col"),
        P(("dp", "row"), "col"),
        P("col"),
        P("col", None, "row"),
        P(None, "row"),
        P("row", "col"),
        P("col"),
        P("col", None, "row"),
        P("row", "col"),
    )
    return jax.shard_map(local, mesh=mesh, in_specs=in_specs, out_specs=out_specs, check_vma=False)
```
